32 devices in a mesh: freq: 8 (over z, x), pair: 4 (over y, core).
Axes of the slice: x: 2, y: 2, z: 4, core: 2. Of those that a mesh axis runs over, the one named last changes fastest.
Arguments:
- samples: bfloat16 [2048, 8, 2, 1024], P(('freq', 'pair')), may hold values from -6 to 6
- rfi_flags: int32 [8, 1024], P('freq'), may hold values 0 or 1
- feed_map: int32 [2048], replicated, may hold values from 0 to 2047, each once
Outputs:
- visibilities: bfloat16 [8, 2, 2048, 2048], P('freq', None, 'pair')
The draws below stay inside these ranges and needn't reach their ends.
Inputs may be any that keep to these rules, and one draw needn't show every extreme that they name: `feed_map`: each of the 2048 feeds is assigned to exactly one slot.
All inputs are finite; a program needn't handle non-finite values. No bound on the sum of `rfi_flags` on one device may be relied on, other than what follows from the above.
Results may differ from the reference program's by a relative error of at most 0.001.
Values may be sent and summed in bfloat16 or wider, within the bound.
No kernel may reach another device: no remote copies, remote signals or barrier semaphores. Data moves between devices by JAX's collectives and lax.ppermute only.
A program may use at most 64 MiB of HBM per device.

```python
import jax
import jax.numpy as jnp
from jax import lax

F = 2048
TS = 1024
CH = 8


def touch_ends(array, stream_key, smallest, largest):
    dims = array.shape
    spot = [jax.random.randint(jax.random.fold_in(stream_key, axis), (), 0, dims[axis]) for axis in range(len(dims))]
    array = array.at[tuple(spot)].set(smallest)
    longest = dims.index(max(dims))
    spot[longest] = (spot[longest] + 1) % dims[longest]
    return array.at[tuple(spot)].set(largest)


def steps_of(own_key, shape, pieces, low, top_value):
    level = 1.0
    for dim, shards_of in pieces:
        steps = jax.random.uniform(jax.random.fold_in(jax.random.fold_in(own_key, 6), dim), (shards_of,), jnp.float32, low / len(pieces), top_value / len(pieces))
        level = level * jnp.repeat(jnp.exp(steps), shape[dim] // shards_of).reshape((-1,) + (1,) * (len(shape) - 1 - dim))
    return level


def gaussian(own_key, extent, scale, reach, split=(), kind=jnp.bfloat16):
    values = scale * jax.random.normal(own_key, extent, jnp.float32)
    if split:
        values = values * steps_of(own_key, extent, split, -0.22, 0.18)
    return jnp.clip(values, -reach, reach).astype(kind)


def setup_inputs(seed: int = 0) -> dict:
    arg_keys = jax.random.split(jax.random.key(seed), 4)
    samples = gaussian(arg_keys[0], (F, CH, 2, TS), 1.0, 6.0, ((0, 32),))
    rfi_flags = touch_ends((jax.random.randint(arg_keys[1], (CH, TS), 0, 4) < 1).astype(jnp.int32), jax.random.fold_in(arg_keys[1], 1), 0, 1)
    feed_map = jax.random.permutation(arg_keys[2], F).astype(jnp.int32)
    return {"samples": samples, "rfi_flags": rfi_flags, "feed_map": feed_map}


def reference(samples, rfi_flags, feed_map):
    keep_mask = (1 - rfi_flags).astype(jnp.bfloat16)

    def channel_vis(channel):
        samples_one = lax.dynamic_index_in_dim(samples, channel, 1, keepdims=False)
        keep_row = lax.dynamic_index_in_dim(keep_mask, channel, 0, keepdims=False)
        flagged = (samples_one * keep_row[None, None, :]).astype(jnp.bfloat16)
        ordered = jnp.take(flagged, feed_map, axis=0)
        parts = ordered.reshape(F, 2 * TS)
        swapped = jnp.concatenate([ordered[:, 1, :], -ordered[:, 0, :]], axis=1)
        stacked = jnp.concatenate([parts, swapped], axis=0)
        product = jnp.dot(stacked, parts.T, preferred_element_type=jnp.float32) * (1.0 / TS)
        return product.reshape(2, F, F).astype(jnp.bfloat16)

    return lax.map(channel_vis, jnp.arange(CH, dtype=jnp.int32))
```

```python
import functools

import jax
import jax.numpy as jnp
from jax import lax
from jax.experimental import pallas as pl
from jax.experimental.pallas import tpu as pltpu
from jax.sharding import PartitionSpec as P

LANES = 128
GROUP = 16
HALVES = 2


def tiles(samples, channel, half, halves):
    feeds, _, _, times = samples.shape
    span = times // halves
    part = lax.dynamic_slice(samples, (0, channel, 0, half * span), (feeds, 1, 2, span))[:, 0]
    blocks = span // LANES
    return part.reshape(feeds, 2, blocks, LANES).transpose(0, 2, 1, 3).reshape(feeds, 2 * blocks, LANES)


def correlate(layout, scale, last, *refs):
    if last:
        place, member, mask, total, *refs = refs
    else:
        place, member, mask, *refs = refs
    pieces, (out, held, ordered, left, sems) = refs[:-5], refs[-5:]
    step = pl.program_id(0)
    rows = left.shape[0] // 2
    deep = held.shape[1]
    block = ordered.shape[0] // pl.num_programs(0)

    @pl.when(step == 0)
    def _():
        copies = []
        for n, (piece, (source, row)) in enumerate(zip(pieces, layout)):
            src = piece if source is None else piece.at[:, pl.ds(source, deep), :]
            copies.append(pltpu.make_async_copy(src, held.at[pl.ds(row, piece.shape[0])], sems.at[n]))
        for copy in copies:
            copy.start()
        for copy in copies:
            copy.wait()

        def gather(group, carry):
            base = pl.multiple_of(group * GROUP, GROUP)
            feeds = jnp.stack([held[place[base + i]] for i in range(GROUP)], 0)
            turned = jnp.transpose(feeds, (1, 0, 2))
            for s in range(deep):
                ordered[pl.ds(base, GROUP), s * LANES : (s + 1) * LANES] = turned[s]
            return carry

        lax.fori_loop(0, ordered.shape[0] // GROUP, gather, 0)
        own = pl.ds(pl.multiple_of(member[0] * rows, GROUP), rows)
        for s in range(deep):
            here = slice(s * LANES, (s + 1) * LANES)
            there = slice((s ^ 1) * LANES, (s ^ 1) * LANES + LANES)
            left[:rows, here] = ordered[own, here] * mask[:, here]
            value = ordered[own, there] * mask[:, here]
            left[rows:, here] = value if s % 2 == 0 else -value

    columns = ordered[pl.ds(pl.multiple_of(step * block, block), block), :]
    product = lax.dot_general(
        left[...], columns, (((1,), (1,)), ((), ())), preferred_element_type=jnp.float32
    )
    if last:
        out[...] = ((product + total[...]) * scale).astype(out.dtype)
    else:
        out[...] = product


def local(samples, rfi_flags, feed_map):
    n_pair, n_freq = lax.axis_size("pair"), lax.axis_size("freq")
    me, member = lax.axis_index("freq"), lax.axis_index("pair")
    feeds, _, _, times = samples.shape
    slots = feed_map.shape[0]
    rows = slots // n_pair

    def over_freq(x, k):
        return lax.ppermute(x, "freq", [(i, i ^ k) for i in range(n_freq)])

    def over_pair(x, k):
        return lax.ppermute(x, "pair", [(i, i ^ k) for i in range(n_pair)])

    near = range(1, n_freq // 2)
    far = [range(k, min(k + 2, n_freq)) for k in range(n_freq // 2, n_freq, 2)]
    groups = []

    def spread(mine, ks, half):
        pieces = {0: mine}
        other = n_pair // 2
        if n_pair > 1:
            pieces[other] = over_pair(mine, other)
            span = 1
            while span < other:
                for m in list(pieces):
                    if m ^ span not in pieces:
                        pieces[m ^ span] = over_pair(pieces[m], span)
                span *= 2
        groups.append((list(ks), half, pieces))

    arrived = {}

    def send(k, half, halves):
        arrived[k, half] = over_freq(tiles(samples, me ^ k, half, halves), k)

    for k in far[0]:
        send(k, 0, HALVES)
    for k in near:
        send(k, 0, 1)
    for half in range(HALVES):
        for ks in far:
            for k in ks:
                if (k, half) not in arrived or (k in near):
                    send(k, half, HALVES)
    own = tiles(samples, me, 0, 1)
    spread(own, [0], None)
    if len(near):
        spread(jnp.concatenate([arrived[k, 0] for k in near]), near, None)
    for half in range(HALVES):
        for ks in far:
            spread(jnp.concatenate([arrived[k, half] for k in ks]), ks, half)

    device, within = feed_map // feeds, feed_map % feeds
    hop, other = (device // n_pair) ^ me, (device % n_pair) ^ member
    keep = (1 - rfi_flags).astype(jnp.bfloat16).reshape(times // LANES, 1, LANES)
    keep = jnp.broadcast_to(keep, (times // LANES, 2, LANES)).reshape(1, 2 * times)
    deep = 2 * times // LANES // HALVES
    total = None
    for half in range(HALVES):
        arrays, layout, row = [], [], 0
        start = {}
        for ks, which, pieces in groups:
            if which is not None and which != half:
                continue
            for m, array in pieces.items():
                arrays.append(array)
                layout.append((None if which is not None else half * deep, row))
                for n, k in enumerate(ks):
                    start[k, m] = row + n * feeds
                row += array.shape[0]
        table = jnp.array([start[k, m] for k in range(n_freq) for m in range(n_pair)], jnp.int32)
        place = table[hop * n_pair + other] + within
        last = half == HALVES - 1
        steps = 8
        width = slots // steps
        mask = keep[:, half * deep * LANES : (half + 1) * deep * LANES]
        smem = pl.BlockSpec(memory_space=pltpu.SMEM)
        block = pl.BlockSpec((2 * rows, width), lambda i: (0, i))
        in_specs = [smem, smem, pl.BlockSpec(mask.shape, lambda i: (0, 0))]
        operands = [place, member.reshape(1), mask]
        if last:
            in_specs.append(block)
            operands.append(total)
        in_specs += [pl.BlockSpec(memory_space=pl.ANY)] * len(arrays)
        total = pl.pallas_call(
            functools.partial(correlate, layout, 1.0 / times, last),
            out_shape=jax.ShapeDtypeStruct((2 * rows, slots), jnp.bfloat16 if last else jnp.float32),
            grid=(steps,),
            in_specs=in_specs,
            out_specs=block,
            scratch_shapes=[
                pltpu.VMEM((slots, deep, LANES), jnp.bfloat16),
                pltpu.VMEM((slots, deep * LANES), jnp.bfloat16),
                pltpu.VMEM((2 * rows, deep * LANES), jnp.bfloat16),
                pltpu.SemaphoreType.DMA((len(arrays),)),
            ],
            compiler_params=pltpu.CompilerParams(vmem_limit_bytes=32 << 20),
        )(*operands, *arrays)
    return total.reshape(1, 2, rows, slots)


def solution(mesh):
    in_specs = (P(("freq", "pair"), None, None, None), P("freq", None), P())
    out_specs = P("freq", None, "pair", None)
    return jax.shard_map(local, mesh=mesh, in_specs=in_specs, out_specs=out_specs, check_vma=False)
```
